32 devices in a mesh: grp: 2 (over y), row: 8 (over z, x), col: 2 (over core).
Axes of the slice: x: 2, y: 2, z: 4, core: 2. Of those that a mesh axis runs over, the one named last changes fastest.
Arguments:
- pair_feats: float32 [32, 16, 192], P(('grp', 'row'), 'col'), parts along dimension 0, may hold values from -6 to 6
- pair_class: int32 [32, 16], P(('grp', 'row'), 'col'), parts along dimension 0, may hold values from 0 to 63
- class_table: float32 [64, 192], replicated, may hold values from -4 to 4
- kernel_one: bfloat16 [3, 3, 192, 192], replicated, may hold values from -0.15625 to 0.15625
- kernel_two: bfloat16 [3, 3, 192, 192], replicated, may hold values from -0.15625 to 0.15625
- norm_gain: float32 [192], replicated, may hold values from 0.1 to 1.9
- w_in: bfloat16 [384, 768], replicated, may hold values from -0.3125 to 0.3125
- w_out: bfloat16 [768, 384], replicated, may hold values from -0.21875 to 0.21875
- partner_perm: int32 [4, 16], replicated, may hold values from 0 to 15, each once within a row
Outputs:
- pair_out: float32 [32, 16, 192], P(('grp', 'row'), 'col'), parts along dimension 0
The draws below stay inside these ranges and needn't reach their ends.
There are 2 independent parts, one for each index of `grp`. The reference program is written for one: setup_inputs(seed, part) draws one part's arguments, and reference() takes and returns one part's arrays. A program takes and returns all parts, laid end to end along the dimension named above; an argument that names none is the same for every part. Nothing has to cross between parts.
Inputs may be any that keep to these rules, and one draw needn't show every extreme that they name: `partner_perm`: each row is a permutation of the 16 cells of a tile.
All inputs are finite; a program needn't handle non-finite values.
Results may differ from the reference program's by a relative error of at most 0.005.
Values may be sent and summed in bfloat16 or wider, within the bound.
A program may use at most 64 MiB of HBM per device.

```python
import jax
import jax.numpy as jnp
from jax import lax

C = 192
HID = 768
CLASSES = 64
TILE_R = 2
TILE_C = 8
CELLS = 16
RBITS = 3
CBITS = 1
LEVELS = 4
NR = 16
NC = 16
N_ROW = 8
N_COL = 2


def set_ends(entries, own_key, low, high):
    index_at = [jax.random.randint(jax.random.fold_in(own_key, axis), (), 0, length) for axis, length in enumerate(entries.shape)]
    widest = entries.shape.index(max(entries.shape))
    neighbour = index_at[:widest] + [(index_at[widest] + 1) % entries.shape[widest]] + index_at[widest + 1:]
    return entries.at[tuple(index_at)].set(low).at[tuple(neighbour)].set(high)


def block_levels(key, dims, shards, least, top_value):
    def one(position, shards_of):
        heights = jax.random.uniform(jax.random.fold_in(jax.random.fold_in(key, 6), position), (shards_of,), jnp.float32, least / len(shards), top_value / len(shards))
        return jnp.repeat(jnp.exp(heights), dims[position] // shards_of).reshape((-1,) + (1,) * (len(dims) - position - 1))

    factor_of = one(*shards[0])
    for cut in shards[1:]:
        factor_of = factor_of * one(*cut)
    return factor_of


def noise(rng, shape, scale, bound, pieces=(), kind=jnp.bfloat16):
    factor_of = block_levels(rng, shape, pieces, -0.22, 0.18) if pieces else 1.0
    values = jax.random.normal(rng, shape, jnp.float32) * scale * factor_of
    return jnp.minimum(jnp.maximum(values, -bound), bound).astype(kind)


def setup_inputs(seed: int = 0, part: int = 0) -> dict:
    key_list = jax.random.split(jax.random.key(seed), 10)
    part_keys = jax.random.split(jax.random.fold_in(key_list[9], part), 10)
    pair_feats = noise(part_keys[0], (NR, NC, C), 1.0, 6.0, ((0, 8), (1, 2)), jnp.float32)
    pair_class = set_ends(jax.random.randint(part_keys[1], (NR, NC), 0, CLASSES), jax.random.fold_in(part_keys[1], 1), 0, CLASSES - 1).astype(jnp.int32)
    class_table = noise(key_list[2], (CLASSES, C), 0.7, 4.0, (), jnp.float32)
    kernel_one = noise(key_list[3], (3, 3, C, C), (9 * C) ** -0.5, 0.15625)
    kernel_two = noise(key_list[4], (3, 3, C, C), (9 * C) ** -0.5, 0.15625)
    norm_gain = jnp.clip(1.0 + 0.18 * jax.random.normal(key_list[5], (C,), jnp.float32), 0.1, 1.9)
    w_in = noise(key_list[6], (2 * C, HID), (2 * C) ** -0.5, 0.3125)
    w_out = noise(key_list[7], (HID, 2 * C), HID ** -0.5, 0.21875)
    partner_perm = jax.vmap(lambda own: jax.random.permutation(own, CELLS))(jax.random.split(key_list[8], LEVELS)).reshape((LEVELS, CELLS)).astype(jnp.int32)
    return dict(pair_feats=pair_feats, pair_class=pair_class, class_table=class_table, kernel_one=kernel_one, kernel_two=kernel_two, norm_gain=norm_gain, w_in=w_in, w_out=w_out, partner_perm=partner_perm)


def convolve(values, kernel):
    rows_all, cols_all, channels = values.shape
    padded = jnp.pad(lax.optimization_barrier(values).astype(jnp.float32), ((1, 1), (1, 1), (0, 0)))
    summed = jnp.zeros((rows_all * cols_all, kernel.shape[3]), jnp.float32)
    for row_shift in range(3):
        for col_shift in range(3):
            window = padded[row_shift:row_shift + rows_all, col_shift:col_shift + cols_all].reshape(rows_all * cols_all, channels)
            summed = summed + jnp.dot(window, kernel[row_shift, col_shift].astype(jnp.float32), precision=lax.Precision.HIGHEST)
    return jnp.maximum(summed, 0.0).reshape(rows_all, cols_all, kernel.shape[3])

def normalize(stream, norm_gain):
    scaled = stream * lax.rsqrt(lax.optimization_barrier(jnp.mean(stream * stream, axis=-1, keepdims=True)) + 1e-05) * norm_gain
    return lax.optimization_barrier(scaled.astype(jnp.bfloat16)).astype(jnp.float32)

def switch_pairs(lower, upper, order, norm_gain, w_in, w_out):
    lower_in = normalize(lower, norm_gain)
    upper_in = normalize(upper, norm_gain)
    pair_units = jnp.concatenate([lower_in, jnp.take(upper_in, order, axis=-2)], axis=-1)
    hidden = jnp.maximum(jnp.matmul(pair_units, w_in.astype(jnp.float32), precision=lax.Precision.HIGHEST), 0.0)
    hidden = lax.optimization_barrier(hidden.astype(jnp.bfloat16)).astype(jnp.float32)
    output = jnp.matmul(hidden, w_out.astype(jnp.float32), precision=lax.Precision.HIGHEST)
    inverse = jnp.zeros_like(order).at[order].set(jnp.arange(CELLS, dtype=jnp.int32))
    new_lower = lower + output[..., :C]
    new_upper = upper + jnp.take(output[..., C:], inverse, axis=-2)
    return (new_lower, new_upper)

def reference(pair_feats, pair_class, class_table, kernel_one, kernel_two, norm_gain, w_in, w_out, partner_perm):
    initial = pair_feats + class_table[pair_class]
    conv_one = convolve(initial.astype(jnp.bfloat16), kernel_one).astype(jnp.bfloat16)
    stream = initial + convolve(conv_one, kernel_two)
    tiles = stream.reshape(N_ROW, TILE_R, N_COL, TILE_C, C).transpose(0, 2, 1, 3, 4).reshape(N_ROW, N_COL, CELLS, C)
    level_index = 0
    for bit_index in range(RBITS):
        stride = 2 ** bit_index
        grouped = tiles.reshape(N_ROW // (2 * stride), 2, stride, N_COL, CELLS, C)
        new_lower, new_upper = switch_pairs(grouped[:, 0], grouped[:, 1], partner_perm[level_index], norm_gain, w_in, w_out)
        tiles = jnp.stack([new_lower, new_upper], axis=1).reshape(N_ROW, N_COL, CELLS, C)
        level_index = level_index + 1
    for bit_index in range(CBITS):
        stride = 2 ** bit_index
        grouped = tiles.reshape(N_ROW, N_COL // (2 * stride), 2, stride, CELLS, C)
        new_lower, new_upper = switch_pairs(grouped[:, :, 0], grouped[:, :, 1], partner_perm[level_index], norm_gain, w_in, w_out)
        tiles = jnp.stack([new_lower, new_upper], axis=2).reshape(N_ROW, N_COL, CELLS, C)
        level_index = level_index + 1
    return tiles.reshape(N_ROW, N_COL, TILE_R, TILE_C, C).transpose(0, 2, 1, 3, 4).reshape(NR, NC, C)
```

```python
import functools

import jax
import jax.numpy as jnp
from jax import lax
from jax.experimental import pallas as pl
from jax.experimental.pallas import tpu as pltpu
from jax.sharding import PartitionSpec as P

MESH = pl.DeviceIdType.MESH


def window_kernel(
    n_row,
    n_col,
    tile_rows,
    tile_cols,
    feats_hbm,
    class_hbm,
    table_hbm,
    one_hbm,
    two_hbm,
    gain_hbm,
    w_in_hbm,
    w_out_hbm,
    perm_hbm,
    out_ref,
    feats,
    classes,
    table,
    kernel_one,
    kernel_two,
    gain,
    w_in,
    w_out,
    perm,
    w_out_half,
    embedded,
    tiles,
    window,
    shifted,
    local_sem,
    send_sem,
    recv_sem,
):
    f32, bf16, i32 = jnp.float32, jnp.bfloat16, jnp.int32
    count = n_row * n_col
    cells = tile_rows * tile_cols
    channels = feats.shape[2]
    width = n_col * tile_cols
    total = count * cells
    row_bits = n_row.bit_length() - 1
    col_bits = n_col.bit_length() - 1
    levels = row_bits + col_bits
    row = lax.axis_index("row")
    col = lax.axis_index("col")
    me = row * n_col + col

    moves = [
        pltpu.make_async_copy(src, dst, local_sem.at[i])
        for i, (src, dst) in enumerate(
            (
                (class_hbm, classes),
                (feats_hbm, feats),
                (table_hbm, table),
                (perm_hbm, perm),
                (w_out_hbm, w_out),
                (one_hbm, kernel_one),
                (two_hbm, kernel_two),
                (gain_hbm, gain),
                (w_in_hbm, w_in),
            )
        )
    ]
    for move in moves[:3]:
        move.start()

    def peer(apart):
        other = lax.rem(me + apart, count)
        return {"row": other // n_col, "col": lax.rem(other, n_col)}

    barrier = pltpu.get_barrier_semaphore()
    for apart in range(1, count):
        pl.semaphore_signal(barrier, inc=1, device_id=peer(apart), device_id_type=MESH)
    for move in moves[3:]:
        move.start()
    for move in moves[:3]:
        move.wait()

    for r in range(tile_rows):
        for c in range(tile_cols):
            embedded[pl.ds(r * tile_cols + c, 1), :] = table[pl.ds(classes[r, c], 1), :]
    initial = feats[...].reshape(cells, channels) + embedded[...]
    rounded = initial.astype(bf16)
    tiles[me] = rounded
    own_rest = initial - rounded.astype(f32)

    pl.semaphore_wait(barrier, count - 1)
    sends = []
    for apart in range(1, count):
        copy = pltpu.make_async_remote_copy(
            src_ref=tiles.at[me],
            dst_ref=tiles.at[me],
            send_sem=send_sem.at[apart - 1],
            recv_sem=recv_sem.at[apart - 1],
            device_id=peer(apart),
            device_id_type=MESH,
        )
        copy.start()
        sends.append(copy)

    moves[3].wait()
    ups = [(row // (1 << bit)) % 2 for bit in range(row_bits)]
    ups += [(col // (1 << bit)) % 2 for bit in range(col_bits)]
    down_iota = lax.broadcasted_iota(i32, (cells, cells), 0)
    across_iota = lax.broadcasted_iota(i32, (cells, cells), 1)
    picks = []
    for level in range(levels):
        upper = jnp.broadcast_to(ups[level], (cells, cells)) == 1
        place = jnp.where(upper, across_iota, down_iota)
        target = jnp.where(upper, down_iota, across_iota)
        value = jnp.zeros((cells, cells), i32)
        for k in range(cells):
            value = jnp.where(place == k, perm[level, k], value)
        picks.append(jnp.where(value == target, 1.0, 0.0).astype(bf16))
    orders = jnp.where(down_iota == across_iota, 1.0, 0.0).astype(bf16)
    for level in reversed(range(levels)):
        turned = jnp.dot(orders, picks[level], preferred_element_type=f32).astype(bf16)
        orders = jnp.concatenate([orders, turned], axis=0)
    cell_iota = lax.broadcasted_iota(i32, (cells, total), 0)
    spot = lax.broadcasted_iota(i32, (cells, total), 1)
    spot_cell = ((spot // width) % tile_rows) * tile_cols + spot % tile_cols
    spread = jnp.where(cell_iota == spot_cell, 1.0, 0.0).astype(bf16)
    order_rows = jnp.dot(orders, spread, preferred_element_type=f32)
    place = lax.broadcasted_iota(i32, (total, 1), 0) // cells
    row_mask = jnp.zeros((total, 1), i32)
    col_mask = jnp.zeros((total, 1), i32)
    for level in range(levels):
        bit = (place >> (levels - 1 - level)) & 1
        if level < row_bits:
            row_mask = row_mask | (bit << level)
        else:
            col_mask = col_mask | (bit << (level - row_bits))
    tile_at = (row ^ row_mask) * n_col + (col ^ col_mask)
    spot_line = lax.broadcasted_iota(i32, (1, total), 1)
    spot_tile = (spot_line // (width * tile_rows)) * n_col + (spot_line % width) // tile_cols
    gather = jnp.where(tile_at == spot_tile, order_rows, 0.0).astype(bf16)

    moves[4].wait()
    w_out_half[0] = w_out[:, :channels]
    w_out_half[1] = w_out[:, channels:]
    edge = jnp.zeros((width, channels), bf16)
    for b in range(3):
        shifted[b, pl.ds(0, width), :] = edge
        shifted[b, pl.ds(width + total, width), :] = edge
    for move in moves[5:]:
        move.wait()

    for copy in sends:
        copy.wait_recv()

    for tile in range(count):
        t, s = divmod(tile, n_col)
        values = tiles[tile].astype(f32)
        for r in range(tile_rows):
            at = (t * tile_rows + r) * width + s * tile_cols
            window[pl.ds(at, tile_cols), :] = values[r * tile_cols : (r + 1) * tile_cols]

    column = lax.broadcasted_iota(i32, (total, 1), 0) % width

    def convolve(values, kernel):
        before = jnp.where(column == 0, 0.0, pltpu.roll(values, 1, 0))
        after = jnp.where(column == width - 1, 0.0, pltpu.roll(values, total - 1, 0))
        for b, part in enumerate((before, values, after)):
            shifted[b, pl.ds(width, total), :] = part.astype(bf16)
        summed = None
        for a in range(3):
            for b in range(3):
                term = jnp.dot(
                    shifted[b, pl.ds(a * width, total), :],
                    kernel[3 * a + b],
                    preferred_element_type=f32,
                )
                summed = term if summed is None else summed + term
        return jnp.maximum(summed, 0.0)

    rounded_window = window[...]
    conv_one = convolve(rounded_window, kernel_one).astype(bf16).astype(f32)
    stream = rounded_window + convolve(conv_one, kernel_two)
    high = stream.astype(bf16)
    low = (stream - high.astype(f32)).astype(bf16)
    stream = jnp.dot(gather, high, preferred_element_type=f32) + jnp.dot(
        gather, low, preferred_element_type=f32
    )
    own_part = stream[:cells] + own_rest
    stream = jnp.concatenate([own_part, stream[cells:]], axis=0)

    size = total
    for level in range(levels):
        normed = (
            stream
            * lax.rsqrt(jnp.mean(stream * stream, axis=-1, keepdims=True) + 1e-05)
            * gain[...]
        ).astype(bf16)
        size = size // 2
        up = ups[level]
        hidden = jnp.dot(normed[:size], w_in[up], preferred_element_type=f32) + jnp.dot(
            normed[size:], w_in[1 - up], preferred_element_type=f32
        )
        hidden = jnp.maximum(hidden, 0.0).astype(bf16)
        stream = stream[:size] + jnp.dot(
            hidden, w_out_half[up], preferred_element_type=f32
        )
    out_ref[...] = stream.reshape(tile_rows, tile_cols, channels)
    for copy in sends:
        copy.wait_send()


def whole_window(
    n_row,
    n_col,
    pair_feats,
    pair_class,
    class_table,
    kernel_one,
    kernel_two,
    norm_gain,
    w_in,
    w_out,
    partner_perm,
):
    tile_rows, tile_cols, channels = pair_feats.shape
    hidden = w_in.shape[1]
    count = n_row * n_col
    cells = tile_rows * tile_cols
    total = count * cells
    width = n_col * tile_cols
    f32, bf16 = jnp.float32, jnp.bfloat16
    anywhere = pl.BlockSpec(memory_space=pltpu.HBM)
    return pl.pallas_call(
        functools.partial(window_kernel, n_row, n_col, tile_rows, tile_cols),
        out_shape=jax.ShapeDtypeStruct(pair_feats.shape, f32),
        in_specs=[anywhere] * 9,
        out_specs=pl.BlockSpec(memory_space=pltpu.VMEM),
        scratch_shapes=[
            pltpu.VMEM(pair_feats.shape, f32),
            pltpu.SMEM(pair_class.shape, jnp.int32),
            pltpu.VMEM(class_table.shape, f32),
            pltpu.VMEM((9, channels, channels), bf16),
            pltpu.VMEM((9, channels, channels), bf16),
            pltpu.VMEM((1, channels), f32),
            pltpu.VMEM((2, channels, hidden), bf16),
            pltpu.VMEM(w_out.shape, bf16),
            pltpu.SMEM(partner_perm.shape, jnp.int32),
            pltpu.VMEM((2, hidden, channels), bf16),
            pltpu.VMEM((cells, channels), f32),
            pltpu.VMEM((count, cells, channels), bf16),
            pltpu.VMEM((total, channels), f32),
            pltpu.VMEM((3, total + 2 * width, channels), bf16),
            pltpu.SemaphoreType.DMA((9,)),
            pltpu.SemaphoreType.DMA((count - 1,)),
            pltpu.SemaphoreType.DMA((count - 1,)),
        ],
        compiler_params=pltpu.CompilerParams(
            collective_id=0, has_side_effects=True, vmem_limit_bytes=48 << 20
        ),
    )(
        pair_feats,
        pair_class,
        class_table,
        kernel_one.reshape(9, channels, channels),
        kernel_two.reshape(9, channels, channels),
        norm_gain.reshape(1, channels),
        w_in.reshape(2, channels, hidden),
        w_out,
        partner_perm,
    )


def with_halo(x, sides, width):
    for axis, dim in sides:
        size, length = (lax.axis_size(axis), x.shape[dim])
        up = [(i, (i + 1) % size) for i in range(size - 1)]
        down = [(j, i) for i, j in up]
        last = lax.slice_in_dim(x, length - width, length, axis=dim)
        first = lax.slice_in_dim(x, 0, width, axis=dim)
        before = lax.ppermute(last, axis, up)
        after = lax.ppermute(first, axis, down)
        x = jnp.concatenate([before, x, after], axis=dim)
    return x


def swapped(block, axis, apart):
    count = lax.axis_size(axis)
    route = []
    for low in range(count):
        high = low | 1 << apart
        if high != low and high < count:
            route += [(low, high), (high, low)]
    return lax.ppermute(block, axis, route)


def convolve(values, kernel):
    tile_rows, tile_cols, channels = values.shape
    padded = with_halo(values, (("row", 0), ("col", 1)), 1)
    summed = jnp.zeros((tile_rows * tile_cols, kernel.shape[3]), jnp.float32)
    for row_shift in range(3):
        for col_shift in range(3):
            window = padded[
                row_shift : row_shift + tile_rows, col_shift : col_shift + tile_cols
            ].reshape(tile_rows * tile_cols, channels)
            summed = summed + jnp.dot(
                window, kernel[row_shift, col_shift], preferred_element_type=jnp.float32
            )
    return jnp.maximum(summed, 0.0)


def axis_position(axis_name):
    if axis_name == "row":
        return lax.axis_index("row")
    return lax.axis_index("col")


def trade_normed(values, axis_name, bit_index):
    if axis_name == "row":
        return swapped(values, "row", bit_index)
    return swapped(values, "col", bit_index)


def switch_level(stream, axis_name, bit_index, order, norm_gain, w_in, w_out):
    cell_count, channels = stream.shape
    upper_flag = axis_position(axis_name) >> bit_index & 1
    is_upper = upper_flag == 1
    scaled = (
        stream * lax.rsqrt(jnp.mean(stream * stream, axis=-1, keepdims=True) + 1e-05) * norm_gain
    )
    normed = scaled.astype(jnp.bfloat16)
    partner = trade_normed(normed, axis_name, bit_index)
    lower_part = jnp.where(is_upper, partner, normed)
    upper_part = jnp.where(is_upper, normed, partner)
    pair_units = jnp.concatenate([lower_part, upper_part[order]], axis=1)
    hidden = jnp.maximum(jnp.dot(pair_units, w_in, preferred_element_type=jnp.float32), 0.0).astype(
        jnp.bfloat16
    )
    out_cols = lax.dynamic_slice_in_dim(w_out, upper_flag * channels, channels, 1)
    update = jnp.dot(hidden, out_cols, preferred_element_type=jnp.float32)
    inverse = jnp.zeros_like(order).at[order].set(jnp.arange(cell_count, dtype=jnp.int32))
    update = jnp.where(is_upper, update[inverse], update)
    return stream + update


def tile_by_tile(
    pair_feats,
    pair_class,
    class_table,
    kernel_one,
    kernel_two,
    norm_gain,
    w_in,
    w_out,
    partner_perm,
):
    tile_rows, tile_cols, channels = pair_feats.shape
    cell_count = tile_rows * tile_cols
    class_count = class_table.shape[0]
    onehot = (
        pair_class.reshape(cell_count, 1) == jnp.arange(class_count, dtype=jnp.int32)[None, :]
    ).astype(jnp.float32)
    embedded = jnp.dot(onehot, class_table, precision=lax.Precision.HIGHEST)
    initial = pair_feats.reshape(cell_count, channels) + embedded
    conv_one = convolve(
        initial.astype(jnp.bfloat16).reshape(tile_rows, tile_cols, channels), kernel_one
    )
    conv_one = conv_one.astype(jnp.bfloat16).reshape(tile_rows, tile_cols, channels)
    stream = initial + convolve(conv_one, kernel_two)
    row_bits = lax.axis_size("row").bit_length() - 1
    level_index = 0
    for bit_index in range(row_bits):
        stream = switch_level(
            stream, "row", bit_index, partner_perm[level_index], norm_gain, w_in, w_out
        )
        level_index = level_index + 1
    bit_index = 0
    stream = switch_level(
        stream, "col", bit_index, partner_perm[level_index], norm_gain, w_in, w_out
    )
    return stream.reshape(tile_rows, tile_cols, channels)


def per_device(n_row, n_col, *operands):
    tile_rows, tile_cols, channels = operands[0].shape
    cells = tile_rows * tile_cols
    window_cells = n_row * n_col * cells
    if window_cells <= 512 and tile_cols % 8 == 0 and cells % 16 == 0:
        return whole_window(n_row, n_col, *operands)
    return tile_by_tile(*operands)


def solution(mesh):
    return jax.shard_map(
        functools.partial(per_device, mesh.shape["row"], mesh.shape["col"]),
        mesh=mesh,
        in_specs=(
            P(("grp", "row"), "col", None),
            P(("grp", "row"), "col"),
            P(),
            P(),
            P(),
            P(),
            P(),
            P(),
            P(),
        ),
        out_specs=P(("grp", "row"), "col", None),
        check_vma=False,
    )
```

```python
import functools

import jax
import jax.numpy as jnp
from jax import lax
from jax.experimental import pallas as pl
from jax.experimental.pallas import tpu as pltpu
from jax.sharding import PartitionSpec as P

MESH = pl.DeviceIdType.MESH


def window_kernel(
    n_row,
    n_col,
    tile_rows,
    tile_cols,
    feats_hbm,
    class_hbm,
    table_hbm,
    one_hbm,
    two_hbm,
    gain_hbm,
    w_in_hbm,
    w_out_hbm,
    perm_hbm,
    out_ref,
    feats,
    classes,
    table,
    kernel_one,
    kernel_two,
    gain,
    w_in,
    w_out,
    perm,
    w_out_half,
    embedded,
    tiles,
    window,
    shifted,
    local_sem,
    send_sem,
    recv_sem,
):
    f32, bf16, i32 = jnp.float32, jnp.bfloat16, jnp.int32
    count = n_row * n_col
    cells = tile_rows * tile_cols
    channels = feats.shape[2]
    width = n_col * tile_cols
    total = count * cells
    row_bits = n_row.bit_length() - 1
    col_bits = n_col.bit_length() - 1
    levels = row_bits + col_bits
    row = lax.axis_index("row")
    col = lax.axis_index("col")
    me = row * n_col + col

    moves = [
        pltpu.make_async_copy(src, dst, local_sem.at[i])
        for i, (src, dst) in enumerate(
            (
                (class_hbm, classes),
                (feats_hbm, feats),
                (table_hbm, table),
                (perm_hbm, perm),
                (w_out_hbm, w_out),
                (one_hbm, kernel_one),
                (two_hbm, kernel_two),
                (gain_hbm, gain),
                (w_in_hbm, w_in),
            )
        )
    ]
    for move in moves[:3]:
        move.start()

    def peer(apart):
        other = lax.rem(me + apart, count)
        return {"row": other // n_col, "col": lax.rem(other, n_col)}

    barrier = pltpu.get_barrier_semaphore()
    for apart in range(1, count):
        pl.semaphore_signal(barrier, inc=1, device_id=peer(apart), device_id_type=MESH)
    for move in moves[3:]:
        move.start()
    for move in moves[:3]:
        move.wait()

    for r in range(tile_rows):
        for c in range(tile_cols):
            embedded[pl.ds(r * tile_cols + c, 1), :] = table[pl.ds(classes[r, c], 1), :]
    initial = feats[...].reshape(cells, channels) + embedded[...]
    rounded = initial.astype(bf16)
    tiles[me] = rounded
    own_rest = initial - rounded.astype(f32)

    pl.semaphore_wait(barrier, count - 1)
    sends = []
    for apart in range(1, count):
        copy = pltpu.make_async_remote_copy(
            src_ref=tiles.at[me],
            dst_ref=tiles.at[me],
            send_sem=send_sem.at[apart - 1],
            recv_sem=recv_sem.at[apart - 1],
            device_id=peer(apart),
            device_id_type=MESH,
        )
        copy.start()
        sends.append(copy)

    moves[3].wait()
    ups = [(row // (1 << bit)) % 2 for bit in range(row_bits)]
    ups += [(col // (1 << bit)) % 2 for bit in range(col_bits)]
    down_iota = lax.broadcasted_iota(i32, (cells, cells), 0)
    across_iota = lax.broadcasted_iota(i32, (cells, cells), 1)
    picks = []
    for level in range(levels):
        upper = jnp.broadcast_to(ups[level], (cells, cells)) == 1
        place = jnp.where(upper, across_iota, down_iota)
        target = jnp.where(upper, down_iota, across_iota)
        value = jnp.zeros((cells, cells), i32)
        for k in range(cells):
            value = jnp.where(place == k, perm[level, k], value)
        picks.append(jnp.where(value == target, 1.0, 0.0).astype(bf16))
    orders = jnp.where(down_iota == across_iota, 1.0, 0.0).astype(bf16)
    for level in reversed(range(levels)):
        turned = jnp.dot(orders, picks[level], preferred_element_type=f32).astype(bf16)
        orders = jnp.concatenate([orders, turned], axis=0)
    cell_iota = lax.broadcasted_iota(i32, (cells, total), 0)
    spot = lax.broadcasted_iota(i32, (cells, total), 1)
    spot_cell = ((spot // width) % tile_rows) * tile_cols + spot % tile_cols
    spread = jnp.where(cell_iota == spot_cell, 1.0, 0.0).astype(bf16)
    order_rows = jnp.dot(orders, spread, preferred_element_type=f32)
    place = lax.broadcasted_iota(i32, (total, 1), 0) // cells
    row_mask = jnp.zeros((total, 1), i32)
    col_mask = jnp.zeros((total, 1), i32)
    for level in range(levels):
        bit = (place >> (levels - 1 - level)) & 1
        if level < row_bits:
            row_mask = row_mask | (bit << level)
        else:
            col_mask = col_mask | (bit << (level - row_bits))
    tile_at = (row ^ row_mask) * n_col + (col ^ col_mask)
    spot_line = lax.broadcasted_iota(i32, (1, total), 1)
    spot_tile = (spot_line // (width * tile_rows)) * n_col + (spot_line % width) // tile_cols
    gather = jnp.where(tile_at == spot_tile, order_rows, 0.0).astype(bf16)

    moves[4].wait()
    w_out_half[0] = w_out[:, :channels]
    w_out_half[1] = w_out[:, channels:]
    edge = jnp.zeros((width, channels), bf16)
    for b in range(3):
        shifted[b, pl.ds(0, width), :] = edge
        shifted[b, pl.ds(width + total, width), :] = edge
    for move in moves[5:]:
        move.wait()

    for copy in sends:
        copy.wait_recv()

    for tile in range(count):
        t, s = divmod(tile, n_col)
        values = tiles[tile].astype(f32)
        for r in range(tile_rows):
            at = (t * tile_rows + r) * width + s * tile_cols
            window[pl.ds(at, tile_cols), :] = values[r * tile_cols : (r + 1) * tile_cols]

    column = lax.broadcasted_iota(i32, (total, 1), 0) % width

    def convolve(values, kernel):
        before = jnp.where(column == 0, 0.0, pltpu.roll(values, 1, 0))
        after = jnp.where(column == width - 1, 0.0, pltpu.roll(values, total - 1, 0))
        for b, part in enumerate((before, values, after)):
            shifted[b, pl.ds(width, total), :] = part.astype(bf16)
        summed = None
        for a in range(3):
            for b in range(3):
                term = jnp.dot(
                    shifted[b, pl.ds(a * width, total), :],
                    kernel[3 * a + b],
                    preferred_element_type=f32,
                )
                summed = term if summed is None else summed + term
        return jnp.maximum(summed, 0.0)

    rounded_window = window[...]
    conv_one = convolve(rounded_window, kernel_one).astype(bf16).astype(f32)
    stream = rounded_window + convolve(conv_one, kernel_two)
    high = stream.astype(bf16)
    low = (stream - high.astype(f32)).astype(bf16)
    stream = jnp.dot(gather, high, preferred_element_type=f32) + jnp.dot(
        gather, low, preferred_element_type=f32
    )
    own_part = stream[:cells] + own_rest
    stream = jnp.concatenate([own_part, stream[cells:]], axis=0)

    size = total
    for level in range(levels):
        normed = (
            stream
            * lax.rsqrt(jnp.mean(stream * stream, axis=-1, keepdims=True) + 1e-05)
            * gain[...]
        ).astype(bf16)
        size = size // 2
        up = ups[level]
        hidden = jnp.dot(normed[:size], w_in[up], preferred_element_type=f32) + jnp.dot(
            normed[size:], w_in[1 - up], preferred_element_type=f32
        )
        hidden = jnp.maximum(hidden, 0.0).astype(bf16)
        stream = stream[:size] + jnp.dot(
            hidden, w_out_half[up], preferred_element_type=f32
        )
    out_ref[...] = stream.reshape(tile_rows, tile_cols, channels)
    for copy in sends:
        copy.wait_send()


def whole_window(
    n_row,
    n_col,
    pair_feats,
    pair_class,
    class_table,
    kernel_one,
    kernel_two,
    norm_gain,
    w_in,
    w_out,
    partner_perm,
):
    tile_rows, tile_cols, channels = pair_feats.shape
    hidden = w_in.shape[1]
    count = n_row * n_col
    cells = tile_rows * tile_cols
    total = count * cells
    width = n_col * tile_cols
    f32, bf16 = jnp.float32, jnp.bfloat16
    anywhere = pl.BlockSpec(memory_space=pltpu.HBM)
    return pl.pallas_call(
        functools.partial(window_kernel, n_row, n_col, tile_rows, tile_cols),
        out_shape=jax.ShapeDtypeStruct(pair_feats.shape, f32),
        in_specs=[anywhere] * 9,
        out_specs=pl.BlockSpec(memory_space=pltpu.VMEM),
        scratch_shapes=[
            pltpu.VMEM(pair_feats.shape, f32),
            pltpu.SMEM(pair_class.shape, jnp.int32),
            pltpu.VMEM(class_table.shape, f32),
            pltpu.VMEM((9, channels, channels), bf16),
            pltpu.VMEM((9, channels, channels), bf16),
            pltpu.VMEM((1, channels), f32),
            pltpu.VMEM((2, channels, hidden), bf16),
            pltpu.VMEM(w_out.shape, bf16),
            pltpu.SMEM(partner_perm.shape, jnp.int32),
            pltpu.VMEM((2, hidden, channels), bf16),
            pltpu.VMEM((cells, channels), f32),
            pltpu.VMEM((count, cells, channels), bf16),
            pltpu.VMEM((total, channels), f32),
            pltpu.VMEM((3, total + 2 * width, channels), bf16),
            pltpu.SemaphoreType.DMA((9,)),
            pltpu.SemaphoreType.DMA((count - 1,)),
            pltpu.SemaphoreType.DMA((count - 1,)),
        ],
        compiler_params=pltpu.CompilerParams(
            collective_id=0, has_side_effects=True, vmem_limit_bytes=62 << 20
        ),
    )(
        pair_feats,
        pair_class,
        class_table,
        kernel_one.reshape(9, channels, channels),
        kernel_two.reshape(9, channels, channels),
        norm_gain.reshape(1, channels),
        w_in.reshape(2, channels, hidden),
        w_out,
        partner_perm,
    )


def with_halo(x, sides, width):
    for axis, dim in sides:
        size, length = (lax.axis_size(axis), x.shape[dim])
        up = [(i, (i + 1) % size) for i in range(size - 1)]
        down = [(j, i) for i, j in up]
        last = lax.slice_in_dim(x, length - width, length, axis=dim)
        first = lax.slice_in_dim(x, 0, width, axis=dim)
        before = lax.ppermute(last, axis, up)
        after = lax.ppermute(first, axis, down)
        x = jnp.concatenate([before, x, after], axis=dim)
    return x


def swapped(block, axis, apart):
    count = lax.axis_size(axis)
    route = []
    for low in range(count):
        high = low | 1 << apart
        if high != low and high < count:
            route += [(low, high), (high, low)]
    return lax.ppermute(block, axis, route)


def convolve(values, kernel):
    tile_rows, tile_cols, channels = values.shape
    padded = with_halo(values, (("row", 0), ("col", 1)), 1)
    summed = jnp.zeros((tile_rows * tile_cols, kernel.shape[3]), jnp.float32)
    for row_shift in range(3):
        for col_shift in range(3):
            window = padded[
                row_shift : row_shift + tile_rows, col_shift : col_shift + tile_cols
            ].reshape(tile_rows * tile_cols, channels)
            summed = summed + jnp.dot(
                window, kernel[row_shift, col_shift], preferred_element_type=jnp.float32
            )
    return jnp.maximum(summed, 0.0)


def axis_position(axis_name):
    if axis_name == "row":
        return lax.axis_index("row")
    return lax.axis_index("col")


def trade_normed(values, axis_name, bit_index):
    if axis_name == "row":
        return swapped(values, "row", bit_index)
    return swapped(values, "col", bit_index)


def switch_level(stream, axis_name, bit_index, order, norm_gain, w_in, w_out):
    cell_count, channels = stream.shape
    upper_flag = axis_position(axis_name) >> bit_index & 1
    is_upper = upper_flag == 1
    scaled = (
        stream * lax.rsqrt(jnp.mean(stream * stream, axis=-1, keepdims=True) + 1e-05) * norm_gain
    )
    normed = scaled.astype(jnp.bfloat16)
    partner = trade_normed(normed, axis_name, bit_index)
    lower_part = jnp.where(is_upper, partner, normed)
    upper_part = jnp.where(is_upper, normed, partner)
    pair_units = jnp.concatenate([lower_part, upper_part[order]], axis=1)
    hidden = jnp.maximum(jnp.dot(pair_units, w_in, preferred_element_type=jnp.float32), 0.0).astype(
        jnp.bfloat16
    )
    out_cols = lax.dynamic_slice_in_dim(w_out, upper_flag * channels, channels, 1)
    update = jnp.dot(hidden, out_cols, preferred_element_type=jnp.float32)
    inverse = jnp.zeros_like(order).at[order].set(jnp.arange(cell_count, dtype=jnp.int32))
    update = jnp.where(is_upper, update[inverse], update)
    return stream + update


def tile_by_tile(
    pair_feats,
    pair_class,
    class_table,
    kernel_one,
    kernel_two,
    norm_gain,
    w_in,
    w_out,
    partner_perm,
):
    tile_rows, tile_cols, channels = pair_feats.shape
    cell_count = tile_rows * tile_cols
    class_count = class_table.shape[0]
    onehot = (
        pair_class.reshape(cell_count, 1) == jnp.arange(class_count, dtype=jnp.int32)[None, :]
    ).astype(jnp.float32)
    embedded = jnp.dot(onehot, class_table, precision=lax.Precision.HIGHEST)
    initial = pair_feats.reshape(cell_count, channels) + embedded
    conv_one = convolve(
        initial.astype(jnp.bfloat16).reshape(tile_rows, tile_cols, channels), kernel_one
    )
    conv_one = conv_one.astype(jnp.bfloat16).reshape(tile_rows, tile_cols, channels)
    stream = initial + convolve(conv_one, kernel_two)
    row_bits = lax.axis_size("row").bit_length() - 1
    level_index = 0
    for bit_index in range(row_bits):
        stream = switch_level(
            stream, "row", bit_index, partner_perm[level_index], norm_gain, w_in, w_out
        )
        level_index = level_index + 1
    bit_index = 0
    stream = switch_level(
        stream, "col", bit_index, partner_perm[level_index], norm_gain, w_in, w_out
    )
    return stream.reshape(tile_rows, tile_cols, channels)


def per_device(n_row, n_col, *operands):
    tile_rows, tile_cols, channels = operands[0].shape
    cells = tile_rows * tile_cols
    window_cells = n_row * n_col * cells
    if window_cells <= 512 and tile_cols % 8 == 0 and cells % 16 == 0:
        return whole_window(n_row, n_col, *operands)
    return tile_by_tile(*operands)


def solution(mesh):
    return jax.shard_map(
        functools.partial(per_device, mesh.shape["row"], mesh.shape["col"]),
        mesh=mesh,
        in_specs=(
            P(("grp", "row"), "col", None),
            P(("grp", "row"), "col"),
            P(),
            P(),
            P(),
            P(),
            P(),
            P(),
            P(),
        ),
        out_specs=P(("grp", "row"), "col", None),
        check_vma=False,
    )
```

```python
import functools

import jax
import jax.numpy as jnp
from jax import lax
from jax.experimental import pallas as pl
from jax.experimental.pallas import tpu as pltpu
from jax.sharding import PartitionSpec as P

MESH = pl.DeviceIdType.MESH


def window_kernel(
    n_row,
    n_col,
    tile_rows,
    tile_cols,
    feats_hbm,
    class_hbm,
    table_hbm,
    one_hbm,
    two_hbm,
    gain_hbm,
    w_in_hbm,
    w_out_hbm,
    perm_hbm,
    out_ref,
    feats,
    classes,
    table,
    kernel_one,
    kernel_two,
    gain,
    w_in,
    w_out,
    perm,
    w_out_half,
    embedded,
    tiles,
    window,
    shifted,
    local_sem,
    send_sem,
    recv_sem,
):
    f32, bf16, i32 = jnp.float32, jnp.bfloat16, jnp.int32
    count = n_row * n_col
    cells = tile_rows * tile_cols
    channels = feats.shape[2]
    width = n_col * tile_cols
    total = count * cells
    row_bits = n_row.bit_length() - 1
    col_bits = n_col.bit_length() - 1
    levels = row_bits + col_bits
    row = lax.axis_index("row")
    col = lax.axis_index("col")
    me = row * n_col + col

    moves = [
        pltpu.make_async_copy(src, dst, local_sem.at[i])
        for i, (src, dst) in enumerate(
            (
                (class_hbm, classes),
                (feats_hbm, feats),
                (table_hbm, table),
                (perm_hbm, perm),
                (w_out_hbm, w_out),
                (one_hbm, kernel_one),
                (two_hbm, kernel_two),
                (gain_hbm, gain),
                (w_in_hbm, w_in),
            )
        )
    ]
    for move in moves[:3]:
        move.start()

    def peer(apart):
        other = lax.rem(me + apart, count)
        return {"row": other // n_col, "col": lax.rem(other, n_col)}

    barrier = pltpu.get_barrier_semaphore()
    for apart in range(1, count):
        pl.semaphore_signal(barrier, inc=1, device_id=peer(apart), device_id_type=MESH)
    for move in moves[3:]:
        move.start()
    for move in moves[:3]:
        move.wait()

    for r in range(tile_rows):
        for c in range(tile_cols):
            embedded[pl.ds(r * tile_cols + c, 1), :] = table[pl.ds(classes[r, c], 1), :]
    initial = feats[...].reshape(cells, channels) + embedded[...]
    rounded = initial.astype(bf16)
    tiles[me] = rounded
    own_rest = initial - rounded.astype(f32)

    pl.semaphore_wait(barrier, count - 1)
    sends = []
    for apart in range(1, count):
        copy = pltpu.make_async_remote_copy(
            src_ref=tiles.at[me],
            dst_ref=tiles.at[me],
            send_sem=send_sem.at[apart - 1],
            recv_sem=recv_sem.at[apart - 1],
            device_id=peer(apart),
            device_id_type=MESH,
        )
        copy.start()
        sends.append(copy)

    moves[3].wait()
    ups = [(row // (1 << bit)) % 2 for bit in range(row_bits)]
    ups += [(col // (1 << bit)) % 2 for bit in range(col_bits)]
    down_iota = lax.broadcasted_iota(i32, (cells, cells), 0)
    across_iota = lax.broadcasted_iota(i32, (cells, cells), 1)
    picks = []
    for level in range(levels):
        upper = jnp.broadcast_to(ups[level], (cells, cells)) == 1
        place = jnp.where(upper, across_iota, down_iota)
        target = jnp.where(upper, down_iota, across_iota)
        value = jnp.zeros((cells, cells), i32)
        for k in range(cells):
            value = jnp.where(place == k, perm[level, k], value)
        picks.append(jnp.where(value == target, 1.0, 0.0).astype(bf16))
    orders = jnp.where(down_iota == across_iota, 1.0, 0.0).astype(bf16)
    for level in reversed(range(levels)):
        turned = jnp.dot(orders, picks[level], preferred_element_type=f32).astype(bf16)
        orders = jnp.concatenate([orders, turned], axis=0)
    cell_iota = lax.broadcasted_iota(i32, (cells, total), 0)
    spot = lax.broadcasted_iota(i32, (cells, total), 1)
    spot_cell = ((spot // width) % tile_rows) * tile_cols + spot % tile_cols
    spread = jnp.where(cell_iota == spot_cell, 1.0, 0.0).astype(bf16)
    order_rows = jnp.dot(orders, spread, preferred_element_type=f32)
    place = lax.broadcasted_iota(i32, (total, 1), 0) // cells
    row_mask = jnp.zeros((total, 1), i32)
    col_mask = jnp.zeros((total, 1), i32)
    for level in range(levels):
        bit = (place >> (levels - 1 - level)) & 1
        if level < row_bits:
            row_mask = row_mask | (bit << level)
        else:
            col_mask = col_mask | (bit << (level - row_bits))
    tile_at = (row ^ row_mask) * n_col + (col ^ col_mask)
    spot_line = lax.broadcasted_iota(i32, (1, total), 1)
    spot_tile = (spot_line // (width * tile_rows)) * n_col + (spot_line % width) // tile_cols
    gather = jnp.where(tile_at == spot_tile, order_rows, 0.0).astype(bf16)

    moves[4].wait()
    w_out_half[0] = w_out[:, :channels]
    w_out_half[1] = w_out[:, channels:]
    edge = jnp.zeros((width, channels), bf16)
    for b in range(3):
        shifted[b, pl.ds(0, width), :] = edge
        shifted[b, pl.ds(width + total, width), :] = edge
    for move in moves[5:]:
        move.wait()

    for copy in sends:
        copy.wait_recv()

    for tile in range(count):
        t, s = divmod(tile, n_col)
        values = tiles[tile].astype(f32)
        for r in range(tile_rows):
            at = (t * tile_rows + r) * width + s * tile_cols
            window[pl.ds(at, tile_cols), :] = values[r * tile_cols : (r + 1) * tile_cols]

    column = lax.broadcasted_iota(i32, (total, 1), 0) % width

    def convolve(values, kernel):
        before = jnp.where(column == 0, 0.0, pltpu.roll(values, 1, 0))
        after = jnp.where(column == width - 1, 0.0, pltpu.roll(values, total - 1, 0))
        for b, part in enumerate((before, values, after)):
            shifted[b, pl.ds(width, total), :] = part.astype(bf16)
        summed = None
        for a in range(3):
            for b in range(3):
                term = jnp.dot(
                    shifted[b, pl.ds(a * width, total), :],
                    kernel[3 * a + b],
                    preferred_element_type=f32,
                )
                summed = term if summed is None else summed + term
        return jnp.maximum(summed, 0.0)

    rounded_window = window[...]
    conv_one = convolve(rounded_window, kernel_one).astype(bf16).astype(f32)
    stream = rounded_window + convolve(conv_one, kernel_two)
    high = stream.astype(bf16)
    low = (stream - high.astype(f32)).astype(bf16)
    stream = jnp.dot(gather, high, preferred_element_type=f32) + jnp.dot(
        gather, low, preferred_element_type=f32
    )
    own_part = stream[:cells] + own_rest
    stream = jnp.concatenate([own_part, stream[cells:]], axis=0)

    size = total
    for level in range(levels):
        scaled = (stream * gain[...]).astype(bf16)
        rate = lax.rsqrt(jnp.mean(stream * stream, axis=-1, keepdims=True) + 1e-05)
        size = size // 2
        up = ups[level]
        hidden = rate[:size] * jnp.dot(
            scaled[:size], w_in[up], preferred_element_type=f32
        ) + rate[size:] * jnp.dot(scaled[size:], w_in[1 - up], preferred_element_type=f32)
        hidden = jnp.maximum(hidden, 0.0).astype(bf16)
        stream = stream[:size] + jnp.dot(
            hidden, w_out_half[up], preferred_element_type=f32
        )
    out_ref[...] = stream.reshape(tile_rows, tile_cols, channels)
    for copy in sends:
        copy.wait_send()


def whole_window(
    n_row,
    n_col,
    pair_feats,
    pair_class,
    class_table,
    kernel_one,
    kernel_two,
    norm_gain,
    w_in,
    w_out,
    partner_perm,
):
    tile_rows, tile_cols, channels = pair_feats.shape
    hidden = w_in.shape[1]
    count = n_row * n_col
    cells = tile_rows * tile_cols
    total = count * cells
    width = n_col * tile_cols
    f32, bf16 = jnp.float32, jnp.bfloat16
    anywhere = pl.BlockSpec(memory_space=pltpu.HBM)
    return pl.pallas_call(
        functools.partial(window_kernel, n_row, n_col, tile_rows, tile_cols),
        out_shape=pltpu.VMEM(pair_feats.shape, f32),
        in_specs=[anywhere] * 9,
        out_specs=pl.BlockSpec(memory_space=pltpu.VMEM),
        scratch_shapes=[
            pltpu.VMEM(pair_feats.shape, f32),
            pltpu.SMEM(pair_class.shape, jnp.int32),
            pltpu.VMEM(class_table.shape, f32),
            pltpu.VMEM((9, channels, channels), bf16),
            pltpu.VMEM((9, channels, channels), bf16),
            pltpu.VMEM((1, channels), f32),
            pltpu.VMEM((2, channels, hidden), bf16),
            pltpu.VMEM(w_out.shape, bf16),
            pltpu.SMEM(partner_perm.shape, jnp.int32),
            pltpu.VMEM((2, hidden, channels), bf16),
            pltpu.VMEM((cells, channels), f32),
            pltpu.VMEM((count, cells, channels), bf16),
            pltpu.VMEM((total, channels), f32),
            pltpu.VMEM((3, total + 2 * width, channels), bf16),
            pltpu.SemaphoreType.DMA((9,)),
            pltpu.SemaphoreType.DMA((count - 1,)),
            pltpu.SemaphoreType.DMA((count - 1,)),
        ],
        compiler_params=pltpu.CompilerParams(
            collective_id=0, has_side_effects=True, vmem_limit_bytes=62 << 20
        ),
    )(
        pair_feats,
        pair_class,
        class_table,
        kernel_one.reshape(9, channels, channels),
        kernel_two.reshape(9, channels, channels),
        norm_gain.reshape(1, channels),
        w_in.reshape(2, channels, hidden),
        w_out,
        partner_perm,
    )


def with_halo(x, sides, width):
    for axis, dim in sides:
        size, length = (lax.axis_size(axis), x.shape[dim])
        up = [(i, (i + 1) % size) for i in range(size - 1)]
        down = [(j, i) for i, j in up]
        last = lax.slice_in_dim(x, length - width, length, axis=dim)
        first = lax.slice_in_dim(x, 0, width, axis=dim)
        before = lax.ppermute(last, axis, up)
        after = lax.ppermute(first, axis, down)
        x = jnp.concatenate([before, x, after], axis=dim)
    return x


def swapped(block, axis, apart):
    count = lax.axis_size(axis)
    route = []
    for low in range(count):
        high = low | 1 << apart
        if high != low and high < count:
            route += [(low, high), (high, low)]
    return lax.ppermute(block, axis, route)


def convolve(values, kernel):
    tile_rows, tile_cols, channels = values.shape
    padded = with_halo(values, (("row", 0), ("col", 1)), 1)
    summed = jnp.zeros((tile_rows * tile_cols, kernel.shape[3]), jnp.float32)
    for row_shift in range(3):
        for col_shift in range(3):
            window = padded[
                row_shift : row_shift + tile_rows, col_shift : col_shift + tile_cols
            ].reshape(tile_rows * tile_cols, channels)
            summed = summed + jnp.dot(
                window, kernel[row_shift, col_shift], preferred_element_type=jnp.float32
            )
    return jnp.maximum(summed, 0.0)


def axis_position(axis_name):
    if axis_name == "row":
        return lax.axis_index("row")
    return lax.axis_index("col")


def trade_normed(values, axis_name, bit_index):
    if axis_name == "row":
        return swapped(values, "row", bit_index)
    return swapped(values, "col", bit_index)


def switch_level(stream, axis_name, bit_index, order, norm_gain, w_in, w_out):
    cell_count, channels = stream.shape
    upper_flag = axis_position(axis_name) >> bit_index & 1
    is_upper = upper_flag == 1
    scaled = (
        stream * lax.rsqrt(jnp.mean(stream * stream, axis=-1, keepdims=True) + 1e-05) * norm_gain
    )
    normed = scaled.astype(jnp.bfloat16)
    partner = trade_normed(normed, axis_name, bit_index)
    lower_part = jnp.where(is_upper, partner, normed)
    upper_part = jnp.where(is_upper, normed, partner)
    pair_units = jnp.concatenate([lower_part, upper_part[order]], axis=1)
    hidden = jnp.maximum(jnp.dot(pair_units, w_in, preferred_element_type=jnp.float32), 0.0).astype(
        jnp.bfloat16
    )
    out_cols = lax.dynamic_slice_in_dim(w_out, upper_flag * channels, channels, 1)
    update = jnp.dot(hidden, out_cols, preferred_element_type=jnp.float32)
    inverse = jnp.zeros_like(order).at[order].set(jnp.arange(cell_count, dtype=jnp.int32))
    update = jnp.where(is_upper, update[inverse], update)
    return stream + update


def tile_by_tile(
    pair_feats,
    pair_class,
    class_table,
    kernel_one,
    kernel_two,
    norm_gain,
    w_in,
    w_out,
    partner_perm,
):
    tile_rows, tile_cols, channels = pair_feats.shape
    cell_count = tile_rows * tile_cols
    class_count = class_table.shape[0]
    onehot = (
        pair_class.reshape(cell_count, 1) == jnp.arange(class_count, dtype=jnp.int32)[None, :]
    ).astype(jnp.float32)
    embedded = jnp.dot(onehot, class_table, precision=lax.Precision.HIGHEST)
    initial = pair_feats.reshape(cell_count, channels) + embedded
    conv_one = convolve(
        initial.astype(jnp.bfloat16).reshape(tile_rows, tile_cols, channels), kernel_one
    )
    conv_one = conv_one.astype(jnp.bfloat16).reshape(tile_rows, tile_cols, channels)
    stream = initial + convolve(conv_one, kernel_two)
    row_bits = lax.axis_size("row").bit_length() - 1
    level_index = 0
    for bit_index in range(row_bits):
        stream = switch_level(
            stream, "row", bit_index, partner_perm[level_index], norm_gain, w_in, w_out
        )
        level_index = level_index + 1
    bit_index = 0
    stream = switch_level(
        stream, "col", bit_index, partner_perm[level_index], norm_gain, w_in, w_out
    )
    return stream.reshape(tile_rows, tile_cols, channels)


def per_device(n_row, n_col, *operands):
    tile_rows, tile_cols, channels = operands[0].shape
    cells = tile_rows * tile_cols
    window_cells = n_row * n_col * cells
    if window_cells <= 512 and tile_cols % 8 == 0 and cells % 16 == 0:
        return whole_window(n_row, n_col, *operands)
    return tile_by_tile(*operands)


def solution(mesh):
    return jax.shard_map(
        functools.partial(per_device, mesh.shape["row"], mesh.shape["col"]),
        mesh=mesh,
        in_specs=(
            P(("grp", "row"), "col", None),
            P(("grp", "row"), "col"),
            P(),
            P(),
            P(),
            P(),
            P(),
            P(),
            P(),
        ),
        out_specs=P(("grp", "row"), "col", None),
        check_vma=False,
    )
```

```python
import functools

import jax
import jax.numpy as jnp
from jax import lax
from jax.experimental import pallas as pl
from jax.experimental.pallas import tpu as pltpu
from jax.sharding import PartitionSpec as P

MESH = pl.DeviceIdType.MESH


def window_kernel(
    n_row,
    n_col,
    tile_rows,
    tile_cols,
    feats_hbm,
    class_hbm,
    table_hbm,
    one_hbm,
    two_hbm,
    gain_hbm,
    w_in_hbm,
    w_out_hbm,
    perm_hbm,
    out_ref,
    feats,
    classes,
    table,
    kernel_one,
    kernel_two,
    gain,
    w_in,
    w_out,
    perm,
    w_out_half,
    embedded,
    tiles,
    window,
    columns,
    shifted,
    local_sem,
    send_sem,
    recv_sem,
):
    f32, bf16, i32 = jnp.float32, jnp.bfloat16, jnp.int32
    count = n_row * n_col
    cells = tile_rows * tile_cols
    channels = feats.shape[2]
    width = n_col * tile_cols
    total = count * cells
    row_bits = n_row.bit_length() - 1
    col_bits = n_col.bit_length() - 1
    levels = row_bits + col_bits
    row = lax.axis_index("row")
    col = lax.axis_index("col")
    me = row * n_col + col

    moves = [
        pltpu.make_async_copy(src, dst, local_sem.at[i])
        for i, (src, dst) in enumerate(
            (
                (class_hbm, classes),
                (feats_hbm, feats),
                (table_hbm, table),
                (perm_hbm, perm),
                (w_out_hbm, w_out),
                (one_hbm, kernel_one),
                (two_hbm, kernel_two),
                (gain_hbm, gain),
                (w_in_hbm, w_in),
            )
        )
    ]
    for move in moves[:3]:
        move.start()

    def peer(apart):
        other = lax.rem(me + apart, count)
        return {"row": other // n_col, "col": lax.rem(other, n_col)}

    barrier = pltpu.get_barrier_semaphore()
    for apart in range(1, count):
        pl.semaphore_signal(barrier, inc=1, device_id=peer(apart), device_id_type=MESH)
    for move in moves[3:]:
        move.start()
    for move in moves[:3]:
        move.wait()

    for r in range(tile_rows):
        for c in range(tile_cols):
            embedded[pl.ds(r * tile_cols + c, 1), :] = table[pl.ds(classes[r, c], 1), :]
    initial = feats[...].reshape(cells, channels) + embedded[...]
    rounded = initial.astype(bf16)
    tiles[me] = rounded
    own_rest = initial - rounded.astype(f32)

    pl.semaphore_wait(barrier, count - 1)
    others = [i + (i - me + count) // count for i in range(count - 1)]
    sends = []
    for i, other in enumerate(others):
        copy = pltpu.make_async_remote_copy(
            src_ref=tiles.at[me],
            dst_ref=tiles.at[me],
            send_sem=send_sem.at[i],
            recv_sem=recv_sem.at[me],
            device_id={"row": other // n_col, "col": lax.rem(other, n_col)},
            device_id_type=MESH,
        )
        copy.start()
        sends.append(copy)

    def arrived(tile):
        pltpu.make_async_remote_copy(
            src_ref=tiles.at[tile],
            dst_ref=tiles.at[tile],
            send_sem=send_sem.at[0],
            recv_sem=recv_sem.at[tile],
            device_id={"row": tile // n_col, "col": lax.rem(tile, n_col)},
            device_id_type=MESH,
        ).wait_recv()

    moves[3].wait()
    ups = [(row // (1 << bit)) % 2 for bit in range(row_bits)]
    ups += [(col // (1 << bit)) % 2 for bit in range(col_bits)]
    down_iota = lax.broadcasted_iota(i32, (cells, cells), 0)
    across_iota = lax.broadcasted_iota(i32, (cells, cells), 1)
    picks = []
    for level in range(levels):
        upper = jnp.broadcast_to(ups[level], (cells, cells)) == 1
        place = jnp.where(upper, across_iota, down_iota)
        target = jnp.where(upper, down_iota, across_iota)
        value = jnp.zeros((cells, cells), i32)
        for k in range(cells):
            value = jnp.where(place == k, perm[level, k], value)
        picks.append(jnp.where(value == target, 1.0, 0.0).astype(bf16))
    orders = jnp.where(down_iota == across_iota, 1.0, 0.0).astype(bf16)
    for level in reversed(range(levels)):
        turned = jnp.dot(orders, picks[level], preferred_element_type=f32).astype(bf16)
        orders = jnp.concatenate([orders, turned], axis=0)
    cell_iota = lax.broadcasted_iota(i32, (cells, total), 0)
    spot = lax.broadcasted_iota(i32, (cells, total), 1)
    spot_cell = ((spot // width) % tile_rows) * tile_cols + spot % tile_cols
    spread = jnp.where(cell_iota == spot_cell, 1.0, 0.0).astype(bf16)
    order_rows = jnp.dot(orders, spread, preferred_element_type=f32)
    place = lax.broadcasted_iota(i32, (total, 1), 0) // cells
    row_mask = jnp.zeros((total, 1), i32)
    col_mask = jnp.zeros((total, 1), i32)
    for level in range(levels):
        bit = (place >> (levels - 1 - level)) & 1
        if level < row_bits:
            row_mask = row_mask | (bit << level)
        else:
            col_mask = col_mask | (bit << (level - row_bits))
    tile_at = (row ^ row_mask) * n_col + (col ^ col_mask)
    spot_line = lax.broadcasted_iota(i32, (1, total), 1)
    spot_tile = (spot_line // (width * tile_rows)) * n_col + (spot_line % width) // tile_cols
    gather = jnp.where(tile_at == spot_tile, order_rows, 0.0).astype(bf16)

    moves[4].wait()
    w_out_half[0] = w_out[:, :channels]
    w_out_half[1] = w_out[:, channels:]
    edge = jnp.zeros((width, channels), bf16)
    for b in range(3):
        shifted[b, pl.ds(0, width), :] = edge
        shifted[b, pl.ds(width + total, width), :] = edge
    for move in moves[5:]:
        move.wait()

    for other in others:
        arrived(other)

    for tile in range(count):
        t, s = divmod(tile, n_col)
        values = tiles[tile].astype(f32)
        for r in range(tile_rows):
            at = (t * tile_rows + r) * width + s * tile_cols
            window[pl.ds(at, tile_cols), :] = values[r * tile_cols : (r + 1) * tile_cols]

    column = lax.broadcasted_iota(i32, (total, 1), 0) % width

    def convolve(values, kernel):
        before = jnp.where(column == 0, 0.0, pltpu.roll(values, 1, 0))
        after = jnp.where(column == width - 1, 0.0, pltpu.roll(values, total - 1, 0))
        for b, part in enumerate((before, values, after)):
            shifted[b, pl.ds(width, total), :] = part.astype(bf16)
        for a in range(3):
            for b in range(3):
                columns[:, pl.ds((3 * a + b) * channels, channels)] = shifted[
                    b, pl.ds(a * width, total), :
                ]
        summed = jnp.dot(columns[...], kernel[...], preferred_element_type=f32)
        return jnp.maximum(summed, 0.0)

    rounded_window = window[...]
    conv_one = convolve(rounded_window, kernel_one).astype(bf16).astype(f32)
    stream = rounded_window + convolve(conv_one, kernel_two)
    high = stream.astype(bf16)
    low = (stream - high.astype(f32)).astype(bf16)
    stream = jnp.dot(gather, high, preferred_element_type=f32)
    own_part = stream[:cells] + (
        jnp.dot(gather[:cells], low, preferred_element_type=f32) + own_rest
    )
    stream = jnp.concatenate([own_part, stream[cells:]], axis=0)

    size = total
    for level in range(levels):
        scaled = (stream * gain[...]).astype(bf16)
        rate = lax.rsqrt(jnp.mean(stream * stream, axis=-1, keepdims=True) + 1e-05)
        size = size // 2
        up = ups[level]
        hidden = rate[:size] * jnp.dot(
            scaled[:size], w_in[up], preferred_element_type=f32
        ) + rate[size:] * jnp.dot(scaled[size:], w_in[1 - up], preferred_element_type=f32)
        hidden = jnp.maximum(hidden, 0.0).astype(bf16)
        stream = stream[:size] + jnp.dot(
            hidden, w_out_half[up], preferred_element_type=f32
        )
    out_ref[...] = stream.reshape(tile_rows, tile_cols, channels)
    for copy in sends:
        copy.wait_send()


def whole_window(
    n_row,
    n_col,
    pair_feats,
    pair_class,
    class_table,
    kernel_one,
    kernel_two,
    norm_gain,
    w_in,
    w_out,
    partner_perm,
):
    tile_rows, tile_cols, channels = pair_feats.shape
    hidden = w_in.shape[1]
    count = n_row * n_col
    cells = tile_rows * tile_cols
    total = count * cells
    width = n_col * tile_cols
    f32, bf16 = jnp.float32, jnp.bfloat16
    anywhere = pl.BlockSpec(memory_space=pltpu.HBM)
    return pl.pallas_call(
        functools.partial(window_kernel, n_row, n_col, tile_rows, tile_cols),
        out_shape=pltpu.VMEM(pair_feats.shape, f32),
        in_specs=[anywhere] * 9,
        out_specs=pl.BlockSpec(memory_space=pltpu.VMEM),
        scratch_shapes=[
            pltpu.VMEM(pair_feats.shape, f32),
            pltpu.SMEM(pair_class.shape, jnp.int32),
            pltpu.VMEM(class_table.shape, f32),
            pltpu.VMEM((9 * channels, channels), bf16),
            pltpu.VMEM((9 * channels, channels), bf16),
            pltpu.VMEM((1, channels), f32),
            pltpu.VMEM((2, channels, hidden), bf16),
            pltpu.VMEM(w_out.shape, bf16),
            pltpu.SMEM(partner_perm.shape, jnp.int32),
            pltpu.VMEM((2, hidden, channels), bf16),
            pltpu.VMEM((cells, channels), f32),
            pltpu.VMEM((count, cells, channels), bf16),
            pltpu.VMEM((total, channels), f32),
            pltpu.VMEM((total, 9 * channels), bf16),
            pltpu.VMEM((3, total + 2 * width, channels), bf16),
            pltpu.SemaphoreType.DMA((9,)),
            pltpu.SemaphoreType.DMA((count - 1,)),
            pltpu.SemaphoreType.DMA((count,)),
        ],
        compiler_params=pltpu.CompilerParams(
            collective_id=0, has_side_effects=True, vmem_limit_bytes=62 << 20
        ),
    )(
        pair_feats,
        pair_class,
        class_table,
        kernel_one.reshape(9 * channels, channels),
        kernel_two.reshape(9 * channels, channels),
        norm_gain.reshape(1, channels),
        w_in.reshape(2, channels, hidden),
        w_out,
        partner_perm,
    )


def with_halo(x, sides, width):
    for axis, dim in sides:
        size, length = (lax.axis_size(axis), x.shape[dim])
        up = [(i, (i + 1) % size) for i in range(size - 1)]
        down = [(j, i) for i, j in up]
        last = lax.slice_in_dim(x, length - width, length, axis=dim)
        first = lax.slice_in_dim(x, 0, width, axis=dim)
        before = lax.ppermute(last, axis, up)
        after = lax.ppermute(first, axis, down)
        x = jnp.concatenate([before, x, after], axis=dim)
    return x


def swapped(block, axis, apart):
    count = lax.axis_size(axis)
    route = []
    for low in range(count):
        high = low | 1 << apart
        if high != low and high < count:
            route += [(low, high), (high, low)]
    return lax.ppermute(block, axis, route)


def convolve(values, kernel):
    tile_rows, tile_cols, channels = values.shape
    padded = with_halo(values, (("row", 0), ("col", 1)), 1)
    summed = jnp.zeros((tile_rows * tile_cols, kernel.shape[3]), jnp.float32)
    for row_shift in range(3):
        for col_shift in range(3):
            window = padded[
                row_shift : row_shift + tile_rows, col_shift : col_shift + tile_cols
            ].reshape(tile_rows * tile_cols, channels)
            summed = summed + jnp.dot(
                window, kernel[row_shift, col_shift], preferred_element_type=jnp.float32
            )
    return jnp.maximum(summed, 0.0)


def axis_position(axis_name):
    if axis_name == "row":
        return lax.axis_index("row")
    return lax.axis_index("col")


def trade_normed(values, axis_name, bit_index):
    if axis_name == "row":
        return swapped(values, "row", bit_index)
    return swapped(values, "col", bit_index)


def switch_level(stream, axis_name, bit_index, order, norm_gain, w_in, w_out):
    cell_count, channels = stream.shape
    upper_flag = axis_position(axis_name) >> bit_index & 1
    is_upper = upper_flag == 1
    scaled = (
        stream * lax.rsqrt(jnp.mean(stream * stream, axis=-1, keepdims=True) + 1e-05) * norm_gain
    )
    normed = scaled.astype(jnp.bfloat16)
    partner = trade_normed(normed, axis_name, bit_index)
    lower_part = jnp.where(is_upper, partner, normed)
    upper_part = jnp.where(is_upper, normed, partner)
    pair_units = jnp.concatenate([lower_part, upper_part[order]], axis=1)
    hidden = jnp.maximum(jnp.dot(pair_units, w_in, preferred_element_type=jnp.float32), 0.0).astype(
        jnp.bfloat16
    )
    out_cols = lax.dynamic_slice_in_dim(w_out, upper_flag * channels, channels, 1)
    update = jnp.dot(hidden, out_cols, preferred_element_type=jnp.float32)
    inverse = jnp.zeros_like(order).at[order].set(jnp.arange(cell_count, dtype=jnp.int32))
    update = jnp.where(is_upper, update[inverse], update)
    return stream + update


def tile_by_tile(
    pair_feats,
    pair_class,
    class_table,
    kernel_one,
    kernel_two,
    norm_gain,
    w_in,
    w_out,
    partner_perm,
):
    tile_rows, tile_cols, channels = pair_feats.shape
    cell_count = tile_rows * tile_cols
    class_count = class_table.shape[0]
    onehot = (
        pair_class.reshape(cell_count, 1) == jnp.arange(class_count, dtype=jnp.int32)[None, :]
    ).astype(jnp.float32)
    embedded = jnp.dot(onehot, class_table, precision=lax.Precision.HIGHEST)
    initial = pair_feats.reshape(cell_count, channels) + embedded
    conv_one = convolve(
        initial.astype(jnp.bfloat16).reshape(tile_rows, tile_cols, channels), kernel_one
    )
    conv_one = conv_one.astype(jnp.bfloat16).reshape(tile_rows, tile_cols, channels)
    stream = initial + convolve(conv_one, kernel_two)
    row_bits = lax.axis_size("row").bit_length() - 1
    level_index = 0
    for bit_index in range(row_bits):
        stream = switch_level(
            stream, "row", bit_index, partner_perm[level_index], norm_gain, w_in, w_out
        )
        level_index = level_index + 1
    bit_index = 0
    stream = switch_level(
        stream, "col", bit_index, partner_perm[level_index], norm_gain, w_in, w_out
    )
    return stream.reshape(tile_rows, tile_cols, channels)


def per_device(n_row, n_col, *operands):
    tile_rows, tile_cols, channels = operands[0].shape
    cells = tile_rows * tile_cols
    window_cells = n_row * n_col * cells
    if window_cells <= 512 and tile_cols % 8 == 0 and cells % 16 == 0:
        return whole_window(n_row, n_col, *operands)
    return tile_by_tile(*operands)


def solution(mesh):
    return jax.shard_map(
        functools.partial(per_device, mesh.shape["row"], mesh.shape["col"]),
        mesh=mesh,
        in_specs=(
            P(("grp", "row"), "col", None),
            P(("grp", "row"), "col"),
            P(),
            P(),
            P(),
            P(),
            P(),
            P(),
            P(),
        ),
        out_specs=P(("grp", "row"), "col", None),
        check_vma=False,
    )
```

```python
import functools

import jax
import jax.numpy as jnp
from jax import lax
from jax.experimental import pallas as pl
from jax.experimental.pallas import tpu as pltpu
from jax.sharding import PartitionSpec as P

MESH = pl.DeviceIdType.MESH


def window_kernel(
    n_row,
    n_col,
    tile_rows,
    tile_cols,
    feats_hbm,
    class_hbm,
    table_hbm,
    one_hbm,
    two_hbm,
    gain_hbm,
    w_in_hbm,
    w_out_hbm,
    perm_hbm,
    out_ref,
    feats,
    classes,
    table,
    kernel_one,
    kernel_two,
    gain,
    w_in,
    w_out,
    perm,
    w_out_half,
    embedded,
    tiles,
    window,
    columns,
    shifted,
    local_sem,
    send_sem,
    recv_sem,
):
    f32, bf16, i32 = jnp.float32, jnp.bfloat16, jnp.int32
    count = n_row * n_col
    cells = tile_rows * tile_cols
    channels = feats.shape[2]
    width = n_col * tile_cols
    total = count * cells
    row_bits = n_row.bit_length() - 1
    col_bits = n_col.bit_length() - 1
    levels = row_bits + col_bits
    row = lax.axis_index("row")
    col = lax.axis_index("col")
    me = row * n_col + col

    moves = [
        pltpu.make_async_copy(src, dst, local_sem.at[i])
        for i, (src, dst) in enumerate(
            (
                (class_hbm, classes),
                (feats_hbm, feats),
                (table_hbm, table),
                (perm_hbm, perm),
                (w_out_hbm, w_out),
                (one_hbm, kernel_one),
                (two_hbm, kernel_two),
                (gain_hbm, gain),
                (w_in_hbm, w_in),
            )
        )
    ]
    for move in moves[:3]:
        move.start()

    others = [i + (i - me + count) // count for i in range(count - 1)]

    def place_of(tile):
        return {"row": tile // n_col, "col": lax.rem(tile, n_col)}

    barrier = pltpu.get_barrier_semaphore()
    for other in others:
        pl.semaphore_signal(barrier, inc=1, device_id=place_of(other), device_id_type=MESH)
    for move in moves[3:]:
        move.start()
    for move in moves[:3]:
        move.wait()

    for r in range(tile_rows):
        for c in range(tile_cols):
            embedded[pl.ds(r * tile_cols + c, 1), :] = table[pl.ds(classes[r, c], 1), :]
    initial = feats[...].reshape(cells, channels) + embedded[...]
    rounded = initial.astype(bf16)
    tiles[me] = rounded
    own_rest = initial - rounded.astype(f32)

    pl.semaphore_wait(barrier, count - 1)
    sends = []
    for i, other in enumerate(others):
        copy = pltpu.make_async_remote_copy(
            src_ref=tiles.at[me],
            dst_ref=tiles.at[me],
            send_sem=send_sem.at[i],
            recv_sem=recv_sem.at[me],
            device_id={"row": other // n_col, "col": lax.rem(other, n_col)},
            device_id_type=MESH,
        )
        copy.start()
        sends.append(copy)

    def arrived(tile):
        pltpu.make_async_remote_copy(
            src_ref=tiles.at[tile],
            dst_ref=tiles.at[tile],
            send_sem=send_sem.at[0],
            recv_sem=recv_sem.at[tile],
            device_id={"row": tile // n_col, "col": lax.rem(tile, n_col)},
            device_id_type=MESH,
        ).wait_recv()

    moves[3].wait()
    ups = [(row // (1 << bit)) % 2 for bit in range(row_bits)]
    ups += [(col // (1 << bit)) % 2 for bit in range(col_bits)]
    down_iota = lax.broadcasted_iota(i32, (cells, cells), 0)
    across_iota = lax.broadcasted_iota(i32, (cells, cells), 1)
    picks = []
    for level in range(levels):
        upper = jnp.broadcast_to(ups[level], (cells, cells)) == 1
        place = jnp.where(upper, across_iota, down_iota)
        target = jnp.where(upper, down_iota, across_iota)
        value = jnp.zeros((cells, cells), i32)
        for k in range(cells):
            value = jnp.where(place == k, perm[level, k], value)
        picks.append(jnp.where(value == target, 1.0, 0.0).astype(bf16))
    orders = jnp.where(down_iota == across_iota, 1.0, 0.0).astype(bf16)
    for level in reversed(range(levels)):
        turned = jnp.dot(orders, picks[level], preferred_element_type=f32).astype(bf16)
        orders = jnp.concatenate([orders, turned], axis=0)
    cell_iota = lax.broadcasted_iota(i32, (cells, total), 0)
    spot = lax.broadcasted_iota(i32, (cells, total), 1)
    spot_cell = ((spot // width) % tile_rows) * tile_cols + spot % tile_cols
    spread = jnp.where(cell_iota == spot_cell, 1.0, 0.0).astype(bf16)
    order_rows = jnp.dot(orders, spread, preferred_element_type=f32)
    place = lax.broadcasted_iota(i32, (total, 1), 0) // cells
    row_mask = jnp.zeros((total, 1), i32)
    col_mask = jnp.zeros((total, 1), i32)
    for level in range(levels):
        bit = (place >> (levels - 1 - level)) & 1
        if level < row_bits:
            row_mask = row_mask | (bit << level)
        else:
            col_mask = col_mask | (bit << (level - row_bits))
    tile_at = (row ^ row_mask) * n_col + (col ^ col_mask)
    spot_line = lax.broadcasted_iota(i32, (1, total), 1)
    spot_tile = (spot_line // (width * tile_rows)) * n_col + (spot_line % width) // tile_cols
    gather = jnp.where(tile_at == spot_tile, order_rows, 0.0).astype(bf16)

    moves[4].wait()
    w_out_half[0] = w_out[:, :channels]
    w_out_half[1] = w_out[:, channels:]
    edge = jnp.zeros((width, channels), bf16)
    for b in range(3):
        shifted[b, pl.ds(0, width), :] = edge
        shifted[b, pl.ds(width + total, width), :] = edge
    for move in moves[5:]:
        move.wait()

    for other in others:
        arrived(other)

    for tile in range(count):
        t, s = divmod(tile, n_col)
        values = tiles[tile].astype(f32)
        for r in range(tile_rows):
            at = (t * tile_rows + r) * width + s * tile_cols
            window[pl.ds(at, tile_cols), :] = values[r * tile_cols : (r + 1) * tile_cols]

    column = lax.broadcasted_iota(i32, (total, 1), 0) % width

    def convolve(values, kernel):
        before = jnp.where(column == 0, 0.0, pltpu.roll(values, 1, 0))
        after = jnp.where(column == width - 1, 0.0, pltpu.roll(values, total - 1, 0))
        for b, part in enumerate((before, values, after)):
            shifted[b, pl.ds(width, total), :] = part.astype(bf16)
        for a in range(3):
            for b in range(3):
                columns[:, pl.ds((3 * a + b) * channels, channels)] = shifted[
                    b, pl.ds(a * width, total), :
                ]
        summed = jnp.dot(columns[...], kernel[...], preferred_element_type=f32)
        return jnp.maximum(summed, 0.0)

    rounded_window = window[...]
    conv_one = convolve(rounded_window, kernel_one).astype(bf16).astype(f32)
    stream = rounded_window + convolve(conv_one, kernel_two)
    high = stream.astype(bf16)
    low = (stream - high.astype(f32)).astype(bf16)
    stream = jnp.dot(gather, high, preferred_element_type=f32)
    own_part = stream[:cells] + (
        jnp.dot(gather[:cells], low, preferred_element_type=f32) + own_rest
    )
    stream = jnp.concatenate([own_part, stream[cells:]], axis=0)

    size = total
    for level in range(levels):
        scaled = (stream * gain[...]).astype(bf16)
        rate = lax.rsqrt(jnp.mean(stream * stream, axis=-1, keepdims=True) + 1e-05)
        size = size // 2
        up = ups[level]
        hidden = rate[:size] * jnp.dot(
            scaled[:size], w_in[up], preferred_element_type=f32
        ) + rate[size:] * jnp.dot(scaled[size:], w_in[1 - up], preferred_element_type=f32)
        hidden = jnp.maximum(hidden, 0.0).astype(bf16)
        stream = stream[:size] + jnp.dot(
            hidden, w_out_half[up], preferred_element_type=f32
        )
    out_ref[...] = stream.reshape(tile_rows, tile_cols, channels)
    for copy in sends:
        copy.wait_send()


def whole_window(
    n_row,
    n_col,
    pair_feats,
    pair_class,
    class_table,
    kernel_one,
    kernel_two,
    norm_gain,
    w_in,
    w_out,
    partner_perm,
):
    tile_rows, tile_cols, channels = pair_feats.shape
    hidden = w_in.shape[1]
    count = n_row * n_col
    cells = tile_rows * tile_cols
    total = count * cells
    width = n_col * tile_cols
    f32, bf16 = jnp.float32, jnp.bfloat16
    anywhere = pl.BlockSpec(memory_space=pltpu.HBM)
    return pl.pallas_call(
        functools.partial(window_kernel, n_row, n_col, tile_rows, tile_cols),
        out_shape=pltpu.VMEM(pair_feats.shape, f32),
        in_specs=[anywhere] * 9,
        out_specs=pl.BlockSpec(memory_space=pltpu.VMEM),
        scratch_shapes=[
            pltpu.VMEM(pair_feats.shape, f32),
            pltpu.SMEM(pair_class.shape, jnp.int32),
            pltpu.VMEM(class_table.shape, f32),
            pltpu.VMEM((9 * channels, channels), bf16),
            pltpu.VMEM((9 * channels, channels), bf16),
            pltpu.VMEM((1, channels), f32),
            pltpu.VMEM((2, channels, hidden), bf16),
            pltpu.VMEM(w_out.shape, bf16),
            pltpu.SMEM(partner_perm.shape, jnp.int32),
            pltpu.VMEM((2, hidden, channels), bf16),
            pltpu.VMEM((cells, channels), f32),
            pltpu.VMEM((count, cells, channels), bf16),
            pltpu.VMEM((total, channels), f32),
            pltpu.VMEM((total, 9 * channels), bf16),
            pltpu.VMEM((3, total + 2 * width, channels), bf16),
            pltpu.SemaphoreType.DMA((9,)),
            pltpu.SemaphoreType.DMA((count - 1,)),
            pltpu.SemaphoreType.DMA((count,)),
        ],
        compiler_params=pltpu.CompilerParams(
            collective_id=0, has_side_effects=True, vmem_limit_bytes=62 << 20
        ),
    )(
        pair_feats,
        pair_class,
        class_table,
        kernel_one.reshape(9 * channels, channels),
        kernel_two.reshape(9 * channels, channels),
        norm_gain.reshape(1, channels),
        w_in.reshape(2, channels, hidden),
        w_out,
        partner_perm,
    )


def with_halo(x, sides, width):
    for axis, dim in sides:
        size, length = (lax.axis_size(axis), x.shape[dim])
        up = [(i, (i + 1) % size) for i in range(size - 1)]
        down = [(j, i) for i, j in up]
        last = lax.slice_in_dim(x, length - width, length, axis=dim)
        first = lax.slice_in_dim(x, 0, width, axis=dim)
        before = lax.ppermute(last, axis, up)
        after = lax.ppermute(first, axis, down)
        x = jnp.concatenate([before, x, after], axis=dim)
    return x


def swapped(block, axis, apart):
    count = lax.axis_size(axis)
    route = []
    for low in range(count):
        high = low | 1 << apart
        if high != low and high < count:
            route += [(low, high), (high, low)]
    return lax.ppermute(block, axis, route)


def convolve(values, kernel):
    tile_rows, tile_cols, channels = values.shape
    padded = with_halo(values, (("row", 0), ("col", 1)), 1)
    summed = jnp.zeros((tile_rows * tile_cols, kernel.shape[3]), jnp.float32)
    for row_shift in range(3):
        for col_shift in range(3):
            window = padded[
                row_shift : row_shift + tile_rows, col_shift : col_shift + tile_cols
            ].reshape(tile_rows * tile_cols, channels)
            summed = summed + jnp.dot(
                window, kernel[row_shift, col_shift], preferred_element_type=jnp.float32
            )
    return jnp.maximum(summed, 0.0)


def axis_position(axis_name):
    if axis_name == "row":
        return lax.axis_index("row")
    return lax.axis_index("col")


def trade_normed(values, axis_name, bit_index):
    if axis_name == "row":
        return swapped(values, "row", bit_index)
    return swapped(values, "col", bit_index)


def switch_level(stream, axis_name, bit_index, order, norm_gain, w_in, w_out):
    cell_count, channels = stream.shape
    upper_flag = axis_position(axis_name) >> bit_index & 1
    is_upper = upper_flag == 1
    scaled = (
        stream * lax.rsqrt(jnp.mean(stream * stream, axis=-1, keepdims=True) + 1e-05) * norm_gain
    )
    normed = scaled.astype(jnp.bfloat16)
    partner = trade_normed(normed, axis_name, bit_index)
    lower_part = jnp.where(is_upper, partner, normed)
    upper_part = jnp.where(is_upper, normed, partner)
    pair_units = jnp.concatenate([lower_part, upper_part[order]], axis=1)
    hidden = jnp.maximum(jnp.dot(pair_units, w_in, preferred_element_type=jnp.float32), 0.0).astype(
        jnp.bfloat16
    )
    out_cols = lax.dynamic_slice_in_dim(w_out, upper_flag * channels, channels, 1)
    update = jnp.dot(hidden, out_cols, preferred_element_type=jnp.float32)
    inverse = jnp.zeros_like(order).at[order].set(jnp.arange(cell_count, dtype=jnp.int32))
    update = jnp.where(is_upper, update[inverse], update)
    return stream + update


def tile_by_tile(
    pair_feats,
    pair_class,
    class_table,
    kernel_one,
    kernel_two,
    norm_gain,
    w_in,
    w_out,
    partner_perm,
):
    tile_rows, tile_cols, channels = pair_feats.shape
    cell_count = tile_rows * tile_cols
    class_count = class_table.shape[0]
    onehot = (
        pair_class.reshape(cell_count, 1) == jnp.arange(class_count, dtype=jnp.int32)[None, :]
    ).astype(jnp.float32)
    embedded = jnp.dot(onehot, class_table, precision=lax.Precision.HIGHEST)
    initial = pair_feats.reshape(cell_count, channels) + embedded
    conv_one = convolve(
        initial.astype(jnp.bfloat16).reshape(tile_rows, tile_cols, channels), kernel_one
    )
    conv_one = conv_one.astype(jnp.bfloat16).reshape(tile_rows, tile_cols, channels)
    stream = initial + convolve(conv_one, kernel_two)
    row_bits = lax.axis_size("row").bit_length() - 1
    level_index = 0
    for bit_index in range(row_bits):
        stream = switch_level(
            stream, "row", bit_index, partner_perm[level_index], norm_gain, w_in, w_out
        )
        level_index = level_index + 1
    bit_index = 0
    stream = switch_level(
        stream, "col", bit_index, partner_perm[level_index], norm_gain, w_in, w_out
    )
    return stream.reshape(tile_rows, tile_cols, channels)


def per_device(n_row, n_col, *operands):
    tile_rows, tile_cols, channels = operands[0].shape
    cells = tile_rows * tile_cols
    window_cells = n_row * n_col * cells
    if window_cells <= 512 and tile_cols % 8 == 0 and cells % 16 == 0:
        return whole_window(n_row, n_col, *operands)
    return tile_by_tile(*operands)


def solution(mesh):
    return jax.shard_map(
        functools.partial(per_device, mesh.shape["row"], mesh.shape["col"]),
        mesh=mesh,
        in_specs=(
            P(("grp", "row"), "col", None),
            P(("grp", "row"), "col"),
            P(),
            P(),
            P(),
            P(),
            P(),
            P(),
            P(),
        ),
        out_specs=P(("grp", "row"), "col", None),
        check_vma=False,
    )
```
